32 devices in a mesh: dp: 16 (over z, x, core), seq: 2 (over y).
Axes of the slice: x: 2, y: 2, z: 4, core: 2. Of those that a mesh axis runs over, the one named last changes fastest.
Arguments:
- queries: bfloat16 [16, 256, 1024], P('dp', 'seq'), may hold values from -6 to 6
- keys: bfloat16 [16, 256, 1024], P('dp', 'seq'), may hold values from -6 to 6
- values: bfloat16 [16, 256, 1024], P('dp', 'seq'), may hold values from -6 to 6
- stream: bfloat16 [16, 256, 1024], P('dp', 'seq'), may hold values from -6 to 6
- cotangent: bfloat16 [16, 256, 1024], P('dp', 'seq'), may hold values from -6 to 6
- attn_out: bfloat16 [1024, 1024], replicated, may hold values from -0.1875 to 0.1875
- point_in: bfloat16 [1024, 2048], replicated, may hold values from -0.1875 to 0.1875
- kernel: bfloat16 [31, 1024], replicated, may hold values from -1 to 1
- point_out: bfloat16 [1024, 1024], replicated, may hold values from -0.1875 to 0.1875
- norm_gain: float32 [1024], replicated, may hold values from 0.1 to 1.9
- conv_gain: float32 [1024], replicated, may hold values from 0.1 to 1.9
- segments: int32 [16, 256], replicated, may hold values from 0 to 127, as said below
- plan: int32 [16], replicated, may hold values from 0 to 15, as said below
Outputs:
- query_grad: bfloat16 [16, 256, 1024], P('dp', 'seq')
- key_grad: bfloat16 [16, 256, 1024], P('dp', 'seq')
- value_grad: bfloat16 [16, 256, 1024], P('dp', 'seq')
- stream_grad: bfloat16 [16, 256, 1024], P('dp', 'seq')
- kernel_grad: float32 [31, 1024], replicated
- proj_grads: float32 [1024, 2048], P(('dp', 'seq'))
The draws below stay inside these ranges and needn't reach their ends.
Inputs may be any that keep to these rules, and one draw needn't show every extreme that they name: `segments`: along each pack the numbers never fall and change only at even frames; one number marks one utterance. `plan`: A permutation of 0 to 15.
All inputs are finite; a program needn't handle non-finite values.
Results may differ from the reference program's by a relative error of at most 0.024.
Values may be sent and summed in bfloat16 or wider, within the bound.
A program may use at most 128 MiB of HBM per device.

```python
import jax
import jax.numpy as jnp
from jax import lax

D = 1024
HEADS = 16
KERNEL = 31
HEAD_DIM = 64
LENGTH = 256
PACKS = 16


def draw_queries(key, part):
    fresh = jnp.clip(jax.random.normal(jax.random.fold_in(key, 1), (PACKS, LENGTH, D)), -6.0, 6.0)
    return fresh.astype(jnp.bfloat16)


def draw_keys(key, part):
    fresh = jnp.clip(jax.random.normal(jax.random.fold_in(key, 2), (PACKS, LENGTH, D)), -6.0, 6.0)
    return fresh.astype(jnp.bfloat16)


def draw_segments(key, part):
    level_key, flag_key = jax.random.split(jax.random.fold_in(key, 3))
    level = jax.random.randint(level_key, (PACKS, 1), 0, 4)
    limits = jnp.array([0, 2048, 16384, 131072], jnp.int32)
    thresh = jnp.sum(jnp.where(level == jnp.arange(4)[None, :], limits[None, :], 0), 1, keepdims=True)
    draws = jax.random.randint(flag_key, (PACKS, LENGTH // 2), 0, 1048576)
    flags = (draws < thresh).astype(jnp.int32) * (jnp.arange(LENGTH // 2) > 0).astype(jnp.int32)[None, :]
    pairs = jnp.cumsum(flags, 1).astype(jnp.int32)
    odd = (jnp.arange(PACKS) % 2).astype(jnp.int32)[:, None]
    lift = (LENGTH // 2 - 1 - pairs[:, -1:]) * odd
    return jnp.repeat(pairs + lift, 2, axis=1).astype(jnp.int32)


def draw_plan(key, part):
    return jax.random.permutation(jax.random.fold_in(key, 5), PACKS).astype(jnp.int32)


def shard_levels(stream_key, extent, cuts, smallest, largest):
    factor_of, own = 1.0, jax.random.fold_in(stream_key, 6)
    for axis_at, parts in cuts:
        heights = jnp.exp(jax.random.uniform(jax.random.fold_in(own, axis_at), (parts,), jnp.float32, smallest / len(cuts), largest / len(cuts)))
        factor_of = factor_of * jnp.repeat(heights, extent[axis_at] // parts).reshape([-1 if axis == axis_at else 1 for axis in range(len(extent))])
    return factor_of


def centred(key, dims, deviation, bound, shards=(), held_as=jnp.bfloat16):
    values = deviation * jax.random.normal(key, dims, jnp.float32)
    if shards:
        values = values * shard_levels(key, dims, shards, -0.22, 0.18)
    return jnp.clip(values, -bound, bound).astype(held_as)


def setup_inputs(seed: int = 0) -> dict:
    splits = jax.random.split(jax.random.key(seed), 14)
    queries = draw_queries(jax.random.fold_in(splits[13], 71), 0)
    keys = draw_keys(jax.random.fold_in(splits[13], 71), 0)
    values = centred(splits[2], (PACKS, LENGTH, D), 1.0, 6.0, ((0, 16), (1, 2)))
    stream = centred(splits[3], (PACKS, LENGTH, D), 1.0, 6.0, ((0, 16), (1, 2)))
    cotangent = centred(splits[4], (PACKS, LENGTH, D), 1.0, 6.0, ((0, 16), (1, 2)))
    attn_out = centred(splits[5], (D, D), D ** -0.5, 0.1875)
    point_in = centred(splits[6], (D, 2 * D), D ** -0.5, 0.1875)
    kernel = centred(splits[7], (KERNEL, D), KERNEL ** -0.5, 1.0)
    point_out = centred(splits[8], (D, D), D ** -0.5, 0.1875)
    norm_gain = jnp.clip(1.0 + 0.18 * jax.random.normal(splits[9], (D,), jnp.float32), 0.1, 1.9)
    conv_gain = jnp.clip(1.0 + 0.18 * jax.random.normal(splits[10], (D,), jnp.float32), 0.1, 1.9)
    segments = draw_segments(jax.random.fold_in(splits[13], 71), 0)
    plan = draw_plan(jax.random.fold_in(splits[13], 71), 0)
    return {"queries": queries, "keys": keys, "values": values, "stream": stream, "cotangent": cotangent, "attn_out": attn_out, "point_in": point_in, "kernel": kernel, "point_out": point_out, "norm_gain": norm_gain, "conv_gain": conv_gain, "segments": segments, "plan": plan}


EPSILON = 1e-05
MASKED = -1e+30

def layer_norm(stream, gain):
    center = lax.optimization_barrier(jnp.mean(stream, -1, keepdims=True))
    shifted = stream - center
    inverse = lax.rsqrt(lax.optimization_barrier(jnp.mean(shifted * shifted, -1, keepdims=True)) + EPSILON)
    normed = shifted * inverse
    return (normed * gain, normed, inverse)

def norm_backward(upstream, normed, inverse, gain):
    scaled = upstream * gain
    return inverse * (scaled - lax.optimization_barrier(jnp.mean(scaled, -1, keepdims=True)) - normed * lax.optimization_barrier(jnp.mean(scaled * normed, -1, keepdims=True)))

def swish_slope(values):
    logistic = jax.nn.sigmoid(values)
    return logistic * (1.0 + values * (1.0 - logistic))

def tap_table(padded_ids, own_ids, taps):
    length = own_ids.shape[0]
    return (jnp.stack([padded_ids[tap:tap + length] for tap in range(taps)], 1) == own_ids[:, None]).astype(jnp.float32)

def depthwise(padded, weights, table):
    length = table.shape[0]
    total = jnp.zeros((length, padded.shape[1]), jnp.float32)
    for tap in range(weights.shape[0]):
        total = total + weights[tap].astype(jnp.float32) * padded[tap:tap + length].astype(jnp.float32) * table[:, tap:tap + 1]
    return total

def tap_sums(upstream, padded, table):
    length = table.shape[0]
    return jnp.stack([lax.optimization_barrier(jnp.sum(upstream * padded[tap:tap + length].astype(jnp.float32) * table[:, tap:tap + 1], 0)) for tap in range(table.shape[1])])

def split_heads(matrix):
    return matrix.reshape(matrix.shape[0], HEADS, HEAD_DIM).transpose(1, 0, 2)

def merge_heads(tensor):
    return tensor.transpose(1, 0, 2).reshape(tensor.shape[1], -1)

def head_weights(query_head, key_head, ids):
    scores = jnp.dot(query_head, key_head.T, preferred_element_type=jnp.float32) * HEAD_DIM ** (-0.5)
    scores = jnp.where(ids[:, None] == ids[None, :], scores, MASKED)
    highest = lax.optimization_barrier(jnp.max(scores, -1, keepdims=True))
    log_total = highest + jnp.log(lax.optimization_barrier(jnp.sum(jnp.exp(scores - highest), -1, keepdims=True)))
    return jnp.exp(scores - log_total)

def pack_pass(queries, keys, values, stream, cotangent, ids, attn_out, point_in, kernel, point_out, norm_gain, conv_gain):

    def forward_head(items):
        query_head, key_head, value_head = items
        weights = head_weights(query_head, key_head, ids)
        return jnp.dot(weights.astype(jnp.bfloat16), value_head, preferred_element_type=jnp.float32).astype(jnp.bfloat16)
    query_heads, key_heads, value_heads = (split_heads(queries), split_heads(keys), split_heads(values))
    mixed = merge_heads(lax.map(forward_head, (query_heads, key_heads, value_heads)))
    hidden = stream.astype(jnp.float32) + jnp.dot(mixed, attn_out, preferred_element_type=jnp.float32)
    normed_in, hat_in, inv_in = layer_norm(hidden, norm_gain)
    both = jnp.dot(normed_in.astype(jnp.bfloat16), point_in, preferred_element_type=jnp.float32)
    linear = both[:, :D]
    logistic = jax.nn.sigmoid(both[:, D:])
    conv_in = (linear * logistic).astype(jnp.bfloat16)
    reach = KERNEL // 2
    padded = jnp.pad(conv_in, ((reach, reach), (0, 0)))
    table = tap_table(jnp.pad(ids, reach, constant_values=-1), ids, KERNEL)
    conv_out = depthwise(padded, kernel, table)
    normed_out, hat_out, inv_out = layer_norm(conv_out, conv_gain)
    activated = (normed_out * jax.nn.sigmoid(normed_out)).astype(jnp.bfloat16)
    act_grad = jnp.dot(cotangent, point_out.T, preferred_element_type=jnp.float32)
    conv_grad = norm_backward(act_grad * swish_slope(normed_out), hat_out, inv_out, conv_gain)
    kernel_part = tap_sums(conv_grad, padded, table)
    in_grad = depthwise(jnp.pad(conv_grad, ((reach, reach), (0, 0))), kernel[::-1], table)
    both_grad = jnp.concatenate([in_grad * logistic, in_grad * linear * logistic * (1.0 - logistic)], 1).astype(jnp.bfloat16)
    back_in = jnp.dot(both_grad, point_in.T, preferred_element_type=jnp.float32)
    stream_out = (cotangent.astype(jnp.float32) + norm_backward(back_in, hat_in, inv_in, norm_gain)).astype(jnp.bfloat16)
    mixed_grad = jnp.dot(stream_out, attn_out.T, preferred_element_type=jnp.float32).astype(jnp.bfloat16)
    scale = HEAD_DIM ** (-0.5)

    def backward_head(items):
        query_head, key_head, value_head, grad_head = items
        weights = head_weights(query_head, key_head, ids)
        slope = jnp.dot(grad_head, value_head.T, preferred_element_type=jnp.float32)
        delta = lax.optimization_barrier(jnp.sum(weights * slope, -1, keepdims=True))
        score_grad = (weights * (slope - delta)).astype(jnp.bfloat16)
        query_part = (jnp.dot(score_grad, key_head, preferred_element_type=jnp.float32) * scale).astype(jnp.bfloat16)
        key_part = (jnp.dot(score_grad.T, query_head, preferred_element_type=jnp.float32) * scale).astype(jnp.bfloat16)
        value_part = jnp.dot(weights.astype(jnp.bfloat16).T, grad_head, preferred_element_type=jnp.float32).astype(jnp.bfloat16)
        return (query_part, key_part, value_part)
    query_part, key_part, value_part = lax.map(backward_head, (query_heads, key_heads, value_heads, split_heads(mixed_grad)))
    proj_part = jnp.concatenate([jnp.dot(mixed.T, stream_out, preferred_element_type=jnp.float32), jnp.dot(activated.T, cotangent, preferred_element_type=jnp.float32)], 1)
    return (merge_heads(query_part), merge_heads(key_part), merge_heads(value_part), stream_out, kernel_part, proj_part)

def reference(queries, keys, values, stream, cotangent, attn_out, point_in, kernel, point_out, norm_gain, conv_gain, segments, plan):

    def one_slot(carry, slot):
        source = plan[slot]
        results = pack_pass(queries[source], keys[source], values[source], stream[source], cotangent[source], segments[source], attn_out, point_in, kernel, point_out, norm_gain, conv_gain)
        return ((carry[0] + results[4], carry[1] + results[5]), (results[0], results[1], results[2], results[3]))
    start = (jnp.zeros((KERNEL, D), jnp.float32), jnp.zeros((D, 2 * D), jnp.float32))
    totals, slots = lax.scan(one_slot, start, jnp.arange(PACKS))
    return (slots[0], slots[1], slots[2], slots[3], totals[0], totals[1])
```

```python
import jax
import jax.numpy as jnp
from jax import lax
from jax.sharding import PartitionSpec as P

HEAD_DIM = 64


EPSILON = 1e-05
MASKED = -1e30


def extended(cells, sides, width):
    for axis, dim in sides:
        count = lax.axis_size(axis)
        ends = count - 1
        head = lax.slice_in_dim(cells, 0, width, axis=dim)
        tail = lax.slice_in_dim(cells, cells.shape[dim] - width, cells.shape[dim], axis=dim)
        cells = jnp.concatenate(
            [
                lax.ppermute(tail, axis, [(i, (i + 1) % count) for i in range(ends)]),
                cells,
                lax.ppermute(head, axis, [((i + 1) % count, i) for i in range(ends)]),
            ],
            axis=dim,
        )
    return cells


def layer_norm(stream, gain):
    center = jnp.mean(stream, -1, keepdims=True)
    shifted = stream - center
    inverse = lax.rsqrt(jnp.mean(shifted * shifted, -1, keepdims=True) + EPSILON)
    normed = shifted * inverse
    return (normed * gain, normed, inverse)


def norm_backward(upstream, normed, inverse, gain):
    scaled = upstream * gain
    return inverse * (
        scaled
        - jnp.mean(scaled, -1, keepdims=True)
        - normed * jnp.mean(scaled * normed, -1, keepdims=True)
    )


def swish_slope(values):
    logistic = jax.nn.sigmoid(values)
    return logistic * (1.0 + values * (1.0 - logistic))


def tap_table(padded_ids, own_ids, taps):
    length = own_ids.shape[0]
    return (
        jnp.stack([padded_ids[tap : tap + length] for tap in range(taps)], 1) == own_ids[:, None]
    ).astype(jnp.float32)


def depthwise(padded, weights, table):
    length = table.shape[0]
    total = jnp.zeros((length, padded.shape[1]), jnp.float32)
    for tap in range(weights.shape[0]):
        total = (
            total
            + weights[tap].astype(jnp.float32)
            * padded[tap : tap + length].astype(jnp.float32)
            * table[:, tap : tap + 1]
        )
    return total


def tap_sums(upstream, padded, table):
    length = table.shape[0]
    return jnp.stack(
        [
            jnp.sum(
                upstream * padded[tap : tap + length].astype(jnp.float32) * table[:, tap : tap + 1],
                0,
            )
            for tap in range(table.shape[1])
        ]
    )


def times_transposed(left, right):
    return lax.dot_general(
        left, right, (((1,), (1,)), ((), ())), preferred_element_type=jnp.float32
    )


def transposed_times(left, right):
    return lax.dot_general(
        left, right, (((0,), (0,)), ((), ())), preferred_element_type=jnp.float32
    )


def split_heads(matrix):
    return matrix.reshape(matrix.shape[0], -1, HEAD_DIM).transpose(1, 0, 2)


def merge_heads(tensor):
    return tensor.transpose(1, 0, 2).reshape(tensor.shape[1], -1)


def shifted_copies(cells, axis):
    count = lax.axis_size(axis)
    return [cells] + [
        lax.ppermute(cells, axis, [((i + step) % count, i) for i in range(count)])
        for step in range(1, count)
    ]


def returned(parts, axis):
    count = lax.axis_size(axis)
    total = parts[0]
    for step in range(1, count):
        back = lax.ppermute(
            parts[step].astype(jnp.bfloat16),
            axis,
            [(i, (i + step) % count) for i in range(count)],
        )
        total = total + back.astype(jnp.float32)
    return total


def route(matrix, plan):
    rows, width = matrix.shape
    slots = plan.shape[0]
    spread = lax.all_to_all(matrix, "dp", split_axis=0, concat_axis=0, tiled=True)
    arranged = jnp.take(spread.reshape(slots, -1, width), plan, axis=0, mode="clip")
    return lax.all_to_all(
        arranged.reshape(rows, width), "dp", split_axis=0, concat_axis=0, tiled=True
    )


def per_device(
    queries,
    keys,
    values,
    stream,
    cotangent,
    attn_out,
    point_in,
    kernel,
    point_out,
    norm_gain,
    conv_gain,
    segments,
    plan,
):
    frames, width = (queries.shape[1], queries.shape[2])
    seq_place = lax.axis_index("seq")
    seq_count = lax.axis_size("seq")
    scale = HEAD_DIM ** (-0.5)
    query_rows, key_rows, value_rows = (queries[0], keys[0], values[0])
    stream_rows, grad_rows = (stream[0], cotangent[0])
    pack_ids = lax.dynamic_index_in_dim(segments, lax.axis_index("dp"), 0, keepdims=False)
    own_ids = lax.dynamic_slice_in_dim(pack_ids, seq_place * frames, frames)
    key_ids = jnp.roll(pack_ids, -seq_place * frames)

    pairs = shifted_copies(jnp.concatenate([key_rows, value_rows], 1), "seq")
    all_pairs = jnp.concatenate(pairs, 0)
    query_heads = split_heads(query_rows)
    key_heads = split_heads(all_pairs[:, :width])
    value_heads = split_heads(all_pairs[:, width:])
    scores = (
        jnp.einsum("hqe,hke->hqk", query_heads, key_heads, preferred_element_type=jnp.float32)
        * scale
    )
    scores = jnp.where((own_ids[:, None] == key_ids[None, :])[None], scores, MASKED)
    highest = jnp.max(scores, -1, keepdims=True)
    raised = jnp.exp(scores - highest)
    weights = raised * (1.0 / jnp.sum(raised, -1, keepdims=True))
    weights_low = weights.astype(jnp.bfloat16)
    mixed = merge_heads(
        jnp.einsum(
            "hqk,hke->hqe", weights_low, value_heads, preferred_element_type=jnp.float32
        ).astype(jnp.bfloat16)
    )
    hidden = stream_rows.astype(jnp.float32) + jnp.dot(
        mixed, attn_out, preferred_element_type=jnp.float32
    )
    normed_in, hat_in, inv_in = layer_norm(hidden, norm_gain)
    both = jnp.dot(normed_in.astype(jnp.bfloat16), point_in, preferred_element_type=jnp.float32)
    linear = both[:, :width]
    logistic = jax.nn.sigmoid(both[:, width:])
    conv_in = (linear * logistic).astype(jnp.bfloat16)
    taps = kernel.shape[0]
    reach = taps // 2
    padded = extended(conv_in, (("seq", 0),), reach)
    padded_ids = lax.dynamic_slice_in_dim(
        jnp.pad(pack_ids, reach, constant_values=-1), seq_place * frames, frames + 2 * reach
    )
    table = tap_table(padded_ids, own_ids, taps)
    conv_out = depthwise(padded, kernel, table)
    normed_out, hat_out, inv_out = layer_norm(conv_out, conv_gain)
    activated = (normed_out * jax.nn.sigmoid(normed_out)).astype(jnp.bfloat16)
    out_part = lax.psum_scatter(
        transposed_times(activated, grad_rows).astype(jnp.bfloat16),
        ("dp", "seq"),
        scatter_dimension=0,
        tiled=True,
    )
    act_grad = times_transposed(grad_rows, point_out)
    conv_grad = norm_backward(act_grad * swish_slope(normed_out), hat_out, inv_out, conv_gain)
    grad_padded = extended(conv_grad.astype(jnp.bfloat16), (("seq", 0),), reach).astype(
        conv_grad.dtype
    )
    kernel_grad = lax.psum(tap_sums(conv_grad, padded, table), ("dp", "seq"))
    in_grad = depthwise(grad_padded, kernel[::-1], table)
    both_grad = jnp.concatenate(
        [in_grad * logistic, in_grad * linear * logistic * (1.0 - logistic)], 1
    ).astype(jnp.bfloat16)
    back_in = times_transposed(both_grad, point_in)
    stream_out = (
        grad_rows.astype(jnp.float32) + norm_backward(back_in, hat_in, inv_in, norm_gain)
    ).astype(jnp.bfloat16)
    in_part = lax.psum_scatter(
        transposed_times(mixed, stream_out).astype(jnp.bfloat16),
        ("dp", "seq"),
        scatter_dimension=0,
        tiled=True,
    )
    mixed_grad = times_transposed(stream_out, attn_out).astype(jnp.bfloat16)
    grad_heads = split_heads(mixed_grad)
    slope = jnp.einsum(
        "hqe,hke->hqk", grad_heads, value_heads, preferred_element_type=jnp.float32
    )
    delta = jnp.sum(weights * slope, -1, keepdims=True)
    score_grad = (weights * (slope - delta)).astype(jnp.bfloat16)
    query_grad = merge_heads(
        (
            jnp.einsum("hqk,hke->hqe", score_grad, key_heads, preferred_element_type=jnp.float32)
            * scale
        ).astype(jnp.bfloat16)
    )
    key_part = merge_heads(
        jnp.einsum("hqk,hqe->hke", score_grad, query_heads, preferred_element_type=jnp.float32)
        * scale
    )
    value_part = merge_heads(
        jnp.einsum("hqk,hqe->hke", weights_low, grad_heads, preferred_element_type=jnp.float32)
    )
    pair_part = jnp.concatenate([key_part, value_part], 1)
    pair_grad = returned(
        [pair_part[step * frames : (step + 1) * frames] for step in range(seq_count)], "seq"
    ).astype(jnp.bfloat16)
    stream_routed = route(stream_out, plan)
    routed = route(jnp.concatenate([query_grad, pair_grad], 1), plan)
    return (
        routed[None, :, :width],
        routed[None, :, width : 2 * width],
        routed[None, :, 2 * width :],
        stream_routed[None],
        kernel_grad,
        jnp.concatenate([in_part, out_part], 1).astype(jnp.float32),
    )


def solution(mesh):
    placed = (
        P("dp", "seq", None),
        P("dp", "seq", None),
        P("dp", "seq", None),
        P("dp", "seq", None),
        P("dp", "seq", None),
        P(),
        P(),
        P(),
        P(),
        P(),
        P(),
        P(),
        P(),
    )
    return jax.shard_map(
        per_device,
        mesh=mesh,
        in_specs=placed,
        out_specs=(
            P("dp", "seq", None),
            P("dp", "seq", None),
            P("dp", "seq", None),
            P("dp", "seq", None),
            P(),
            P(("dp", "seq"), None),
        ),
        check_vma=False,
    )
```

```python
import jax
import jax.numpy as jnp
from jax import lax
from jax.sharding import PartitionSpec as P

HEAD_DIM = 64


EPSILON = 1e-05
MASKED = -1e30


def extended(cells, sides, width):
    for axis, dim in sides:
        count = lax.axis_size(axis)
        ends = count - 1
        head = lax.slice_in_dim(cells, 0, width, axis=dim)
        tail = lax.slice_in_dim(cells, cells.shape[dim] - width, cells.shape[dim], axis=dim)
        cells = jnp.concatenate(
            [
                lax.ppermute(tail, axis, [(i, (i + 1) % count) for i in range(ends)]),
                cells,
                lax.ppermute(head, axis, [((i + 1) % count, i) for i in range(ends)]),
            ],
            axis=dim,
        )
    return cells


def layer_norm(stream, gain):
    center = jnp.mean(stream, -1, keepdims=True)
    shifted = stream - center
    inverse = lax.rsqrt(jnp.mean(shifted * shifted, -1, keepdims=True) + EPSILON)
    normed = shifted * inverse
    return (normed * gain, normed, inverse)


def norm_backward(upstream, normed, inverse, gain):
    scaled = upstream * gain
    return inverse * (
        scaled
        - jnp.mean(scaled, -1, keepdims=True)
        - normed * jnp.mean(scaled * normed, -1, keepdims=True)
    )


def swish_slope(values):
    logistic = jax.nn.sigmoid(values)
    return logistic * (1.0 + values * (1.0 - logistic))


def tap_table(padded_ids, own_ids, taps):
    length = own_ids.shape[0]
    return (
        jnp.stack([padded_ids[tap : tap + length] for tap in range(taps)], 1) == own_ids[:, None]
    ).astype(jnp.float32)


def depthwise(padded, weights, table):
    length = table.shape[0]
    total = jnp.zeros((length, padded.shape[1]), jnp.float32)
    for tap in range(weights.shape[0]):
        total = (
            total
            + weights[tap].astype(jnp.float32)
            * padded[tap : tap + length].astype(jnp.float32)
            * table[:, tap : tap + 1]
        )
    return total


def tap_sums(upstream, padded, table):
    length = table.shape[0]
    return jnp.stack(
        [
            jnp.sum(
                upstream * padded[tap : tap + length].astype(jnp.float32) * table[:, tap : tap + 1],
                0,
            )
            for tap in range(table.shape[1])
        ]
    )


def times_transposed(left, right):
    return lax.dot_general(
        left, right, (((1,), (1,)), ((), ())), preferred_element_type=jnp.float32
    )


def transposed_times(left, right):
    return lax.dot_general(
        left, right, (((0,), (0,)), ((), ())), preferred_element_type=jnp.float32
    )


def split_heads(matrix):
    return matrix.reshape(matrix.shape[0], -1, HEAD_DIM).transpose(1, 0, 2)


def merge_heads(tensor):
    return tensor.transpose(1, 0, 2).reshape(tensor.shape[1], -1)


def shifted_copies(cells, axis):
    count = lax.axis_size(axis)
    return [cells] + [
        lax.ppermute(cells, axis, [((i + step) % count, i) for i in range(count)])
        for step in range(1, count)
    ]


def returned(parts, axis):
    count = lax.axis_size(axis)
    total = parts[0]
    for step in range(1, count):
        back = lax.ppermute(
            parts[step].astype(jnp.bfloat16),
            axis,
            [(i, (i + step) % count) for i in range(count)],
        )
        total = total + back.astype(jnp.float32)
    return total


def route(matrix, plan):
    rows, width = matrix.shape
    slots = plan.shape[0]
    spread = lax.all_to_all(matrix, "dp", split_axis=0, concat_axis=0, tiled=True)
    arranged = jnp.take(spread.reshape(slots, -1, width), plan, axis=0, mode="clip")
    return lax.all_to_all(
        arranged.reshape(rows, width), "dp", split_axis=0, concat_axis=0, tiled=True
    )


def exchange_order():
    slots = (lax.axis_size("dp") - 1).bit_length()
    seqs = (lax.axis_size("seq") - 1).bit_length()
    return (
        [("dp", bit, seqs + bit) for bit in range(min(2, slots))]
        + [("seq", bit, bit) for bit in range(seqs)]
        + [("dp", bit, seqs + bit) for bit in range(2, slots)]
    )


def swapped(cells, axis, bit):
    return lax.ppermute(
        cells, axis, [(i, i ^ (1 << bit)) for i in range(lax.axis_size(axis))]
    )


def reduced_product(left, right):
    order = exchange_order()
    blocks = 1 << len(order)
    rows = left.shape[1] // blocks
    positions = sorted(position for _, _, position in order)
    total = None
    for axis, bit, position in order:
        low = rows << positions.index(position)
        positions.remove(position)
        mine = (lax.axis_index(axis) >> bit) & 1
        if total is None:
            split = left.reshape(left.shape[0], -1, 2, low)

            def piece(which):
                chosen = lax.dynamic_index_in_dim(split, which, 2, keepdims=False)
                return transposed_times(chosen.reshape(left.shape[0], -1), right)

        else:
            split = total.reshape(-1, 2, low, right.shape[1])

            def piece(which):
                chosen = lax.dynamic_index_in_dim(split, which, 1, keepdims=False)
                return chosen.reshape(-1, right.shape[1])

        arrived = swapped(piece(1 - mine).astype(jnp.bfloat16), axis, bit)
        total = piece(mine) + arrived.astype(jnp.float32)
    return total


def reduced_everywhere(cells):
    for axis, bit, _ in exchange_order():
        cells = cells + swapped(cells, axis, bit)
    return cells


def per_device(
    queries,
    keys,
    values,
    stream,
    cotangent,
    attn_out,
    point_in,
    kernel,
    point_out,
    norm_gain,
    conv_gain,
    segments,
    plan,
):
    frames, width = (queries.shape[1], queries.shape[2])
    seq_place = lax.axis_index("seq")
    seq_count = lax.axis_size("seq")
    scale = HEAD_DIM ** (-0.5)
    query_rows, key_rows, value_rows = (queries[0], keys[0], values[0])
    stream_rows, grad_rows = (stream[0], cotangent[0])
    pack_ids = lax.dynamic_index_in_dim(segments, lax.axis_index("dp"), 0, keepdims=False)
    own_ids = lax.dynamic_slice_in_dim(pack_ids, seq_place * frames, frames)
    key_ids = jnp.roll(pack_ids, -seq_place * frames)

    pairs = shifted_copies(jnp.concatenate([key_rows, value_rows], 1), "seq")
    all_pairs = jnp.concatenate(pairs, 0)
    query_heads = split_heads(query_rows)
    key_heads = split_heads(all_pairs[:, :width])
    value_heads = split_heads(all_pairs[:, width:])
    scores = (
        jnp.einsum("hqe,hke->hqk", query_heads, key_heads, preferred_element_type=jnp.float32)
        * scale
    )
    scores = jnp.where((own_ids[:, None] == key_ids[None, :])[None], scores, MASKED)
    highest = jnp.max(scores, -1, keepdims=True)
    raised = jnp.exp(scores - highest)
    weights = raised * (1.0 / jnp.sum(raised, -1, keepdims=True))
    weights_low = weights.astype(jnp.bfloat16)
    mixed = merge_heads(
        jnp.einsum(
            "hqk,hke->hqe", weights_low, value_heads, preferred_element_type=jnp.float32
        ).astype(jnp.bfloat16)
    )
    hidden = stream_rows.astype(jnp.float32) + jnp.dot(
        mixed, attn_out, preferred_element_type=jnp.float32
    )
    normed_in, hat_in, inv_in = layer_norm(hidden, norm_gain)
    both = jnp.dot(normed_in.astype(jnp.bfloat16), point_in, preferred_element_type=jnp.float32)
    linear = both[:, :width]
    logistic = jax.nn.sigmoid(both[:, width:])
    conv_in = (linear * logistic).astype(jnp.bfloat16)
    taps = kernel.shape[0]
    reach = taps // 2
    padded = extended(conv_in, (("seq", 0),), reach)
    padded_ids = lax.dynamic_slice_in_dim(
        jnp.pad(pack_ids, reach, constant_values=-1), seq_place * frames, frames + 2 * reach
    )
    table = tap_table(padded_ids, own_ids, taps)
    conv_out = depthwise(padded, kernel, table)
    normed_out, hat_out, inv_out = layer_norm(conv_out, conv_gain)
    activated = (normed_out * jax.nn.sigmoid(normed_out)).astype(jnp.bfloat16)
    out_part = reduced_product(activated, grad_rows)
    act_grad = times_transposed(grad_rows, point_out)
    conv_grad = norm_backward(act_grad * swish_slope(normed_out), hat_out, inv_out, conv_gain)
    grad_padded = extended(conv_grad.astype(jnp.bfloat16), (("seq", 0),), reach).astype(
        conv_grad.dtype
    )
    kernel_grad = reduced_everywhere(tap_sums(conv_grad, padded, table))
    in_grad = depthwise(grad_padded, kernel[::-1], table)
    both_grad = jnp.concatenate(
        [in_grad * logistic, in_grad * linear * logistic * (1.0 - logistic)], 1
    ).astype(jnp.bfloat16)
    back_in = times_transposed(both_grad, point_in)
    stream_out = (
        grad_rows.astype(jnp.float32) + norm_backward(back_in, hat_in, inv_in, norm_gain)
    ).astype(jnp.bfloat16)
    in_part = reduced_product(mixed, stream_out)
    mixed_grad = times_transposed(stream_out, attn_out).astype(jnp.bfloat16)
    grad_heads = split_heads(mixed_grad)
    slope = jnp.einsum(
        "hqe,hke->hqk", grad_heads, value_heads, preferred_element_type=jnp.float32
    )
    delta = jnp.sum(weights * slope, -1, keepdims=True)
    score_grad = (weights * (slope - delta)).astype(jnp.bfloat16)
    query_grad = merge_heads(
        (
            jnp.einsum("hqk,hke->hqe", score_grad, key_heads, preferred_element_type=jnp.float32)
            * scale
        ).astype(jnp.bfloat16)
    )
    key_part = merge_heads(
        jnp.einsum("hqk,hqe->hke", score_grad, query_heads, preferred_element_type=jnp.float32)
        * scale
    )
    value_part = merge_heads(
        jnp.einsum("hqk,hqe->hke", weights_low, grad_heads, preferred_element_type=jnp.float32)
    )
    pair_part = jnp.concatenate([key_part, value_part], 1)
    pair_grad = returned(
        [pair_part[step * frames : (step + 1) * frames] for step in range(seq_count)], "seq"
    ).astype(jnp.bfloat16)
    stream_routed = route(stream_out, plan)
    routed = route(jnp.concatenate([query_grad, pair_grad], 1), plan)
    return (
        routed[None, :, :width],
        routed[None, :, width : 2 * width],
        routed[None, :, 2 * width :],
        stream_routed[None],
        kernel_grad,
        jnp.concatenate([in_part, out_part], 1),
    )


def solution(mesh):
    placed = (
        P("dp", "seq", None),
        P("dp", "seq", None),
        P("dp", "seq", None),
        P("dp", "seq", None),
        P("dp", "seq", None),
        P(),
        P(),
        P(),
        P(),
        P(),
        P(),
        P(),
        P(),
    )
    return jax.shard_map(
        per_device,
        mesh=mesh,
        in_specs=placed,
        out_specs=(
            P("dp", "seq", None),
            P("dp", "seq", None),
            P("dp", "seq", None),
            P("dp", "seq", None),
            P(),
            P(("dp", "seq"), None),
        ),
        check_vma=False,
    )
```

```python
import jax
import jax.numpy as jnp
from jax import lax
from jax.sharding import PartitionSpec as P

HEAD_DIM = 64


EPSILON = 1e-05
MASKED = -1e30


def extended(cells, sides, width):
    for axis, dim in sides:
        count = lax.axis_size(axis)
        ends = count - 1
        head = lax.slice_in_dim(cells, 0, width, axis=dim)
        tail = lax.slice_in_dim(cells, cells.shape[dim] - width, cells.shape[dim], axis=dim)
        cells = jnp.concatenate(
            [
                lax.ppermute(tail, axis, [(i, (i + 1) % count) for i in range(ends)]),
                cells,
                lax.ppermute(head, axis, [((i + 1) % count, i) for i in range(ends)]),
            ],
            axis=dim,
        )
    return cells


def layer_norm(stream, gain):
    center = jnp.mean(stream, -1, keepdims=True)
    shifted = stream - center
    inverse = lax.rsqrt(jnp.mean(shifted * shifted, -1, keepdims=True) + EPSILON)
    normed = shifted * inverse
    return (normed * gain, normed, inverse)


def norm_backward(upstream, normed, inverse, gain):
    scaled = upstream * gain
    return inverse * (
        scaled
        - jnp.mean(scaled, -1, keepdims=True)
        - normed * jnp.mean(scaled * normed, -1, keepdims=True)
    )


def swish_slope(values):
    logistic = jax.nn.sigmoid(values)
    return logistic * (1.0 + values * (1.0 - logistic))


def tap_table(padded_ids, own_ids, taps):
    length = own_ids.shape[0]
    return (
        jnp.stack([padded_ids[tap : tap + length] for tap in range(taps)], 1) == own_ids[:, None]
    ).astype(jnp.float32)


def depthwise(padded, weights, table):
    length = table.shape[0]
    total = jnp.zeros((length, padded.shape[1]), jnp.float32)
    for tap in range(weights.shape[0]):
        total = (
            total
            + weights[tap].astype(jnp.float32)
            * padded[tap : tap + length].astype(jnp.float32)
            * table[:, tap : tap + 1]
        )
    return total


def tap_sums(upstream, padded, table):
    length = table.shape[0]
    return jnp.stack(
        [
            jnp.sum(
                upstream * padded[tap : tap + length].astype(jnp.float32) * table[:, tap : tap + 1],
                0,
            )
            for tap in range(table.shape[1])
        ]
    )


def times_transposed(left, right):
    return lax.dot_general(
        left, right, (((1,), (1,)), ((), ())), preferred_element_type=jnp.float32
    )


def transposed_times(left, right):
    return lax.dot_general(
        left, right, (((0,), (0,)), ((), ())), preferred_element_type=jnp.float32
    )


def split_heads(matrix):
    return matrix.reshape(matrix.shape[0], -1, HEAD_DIM).transpose(1, 0, 2)


def merge_heads(tensor):
    return tensor.transpose(1, 0, 2).reshape(tensor.shape[1], -1)


def shifted_copies(cells, axis):
    count = lax.axis_size(axis)
    return [cells] + [
        lax.ppermute(cells, axis, [((i + step) % count, i) for i in range(count)])
        for step in range(1, count)
    ]


def returned(parts, axis):
    count = lax.axis_size(axis)
    total = parts[0]
    for step in range(1, count):
        back = lax.ppermute(
            parts[step].astype(jnp.bfloat16),
            axis,
            [(i, (i + step) % count) for i in range(count)],
        )
        total = total + back.astype(jnp.float32)
    return total


def spread_rows(matrix):
    return lax.all_to_all(matrix, "dp", split_axis=0, concat_axis=0, tiled=True)


def collected(spread, plan):
    rows, width = spread.shape
    arranged = jnp.take(spread.reshape(plan.shape[0], -1, width), plan, axis=0, mode="clip")
    return spread_rows(arranged.reshape(rows, width))


def route(matrix, plan):
    return collected(spread_rows(matrix), plan)


def exchange_order():
    slots = (lax.axis_size("dp") - 1).bit_length()
    seqs = (lax.axis_size("seq") - 1).bit_length()
    return (
        [("dp", bit, seqs + bit) for bit in range(min(1, slots))]
        + [("seq", bit, bit) for bit in range(seqs)]
        + [("dp", bit, seqs + bit) for bit in range(1, slots)]
    )


def swapped(cells, axis, bit):
    return lax.ppermute(
        cells, axis, [(i, i ^ (1 << bit)) for i in range(lax.axis_size(axis))]
    )


def half_of(cells, dim, low, which):
    shape = cells.shape
    split = cells.reshape(shape[:dim] + (-1, 2, low) + shape[dim + 1 :])
    chosen = lax.dynamic_index_in_dim(split, which, dim + 1, keepdims=False)
    return chosen.reshape(shape[:dim] + (-1,) + shape[dim + 1 :])


def joined(axis, bit, outgoing, extra):
    outgoing = outgoing.astype(jnp.bfloat16)
    if extra is None:
        return swapped(outgoing, axis, bit).astype(jnp.float32), None
    rounded = lax.reduce_precision(extra, 8, 7)
    arrived = swapped(
        jnp.concatenate([outgoing, rounded.astype(jnp.bfloat16)], 0), axis, bit
    ).astype(jnp.float32)
    count = outgoing.shape[0]
    return arrived[:count], rounded + arrived[count:]


class Reduction:
    def __init__(self, left, right, extra=None):
        self.order = exchange_order()
        self.rows = left.shape[1] >> len(self.order)
        self.positions = sorted(position for _, _, position in self.order)
        self.extra = extra
        axis, bit, low, mine = self.next_exchange()
        outgoing = transposed_times(half_of(left, 1, low, 1 - mine), right)
        arrived, self.extra = joined(axis, bit, outgoing, self.extra)
        self.total = transposed_times(half_of(left, 1, low, mine), right) + arrived

    def next_exchange(self):
        axis, bit, position = self.order.pop(0)
        low = self.rows << self.positions.index(position)
        self.positions.remove(position)
        return axis, bit, low, (lax.axis_index(axis) >> bit) & 1

    def step(self):
        if self.order:
            axis, bit, low, mine = self.next_exchange()
            outgoing = half_of(self.total, 0, low, 1 - mine)
            arrived, self.extra = joined(axis, bit, outgoing, self.extra)
            self.total = half_of(self.total, 0, low, mine) + arrived

    def finish(self):
        while self.order:
            self.step()
        return self.total

    def tie(self, other):
        self.total, other = lax.optimization_barrier((self.total, other))
        return other


def per_device(
    queries,
    keys,
    values,
    stream,
    cotangent,
    attn_out,
    point_in,
    kernel,
    point_out,
    norm_gain,
    conv_gain,
    segments,
    plan,
):
    frames, width = (queries.shape[1], queries.shape[2])
    seq_place = lax.axis_index("seq")
    seq_count = lax.axis_size("seq")
    scale = HEAD_DIM ** (-0.5)
    query_rows, key_rows, value_rows = (queries[0], keys[0], values[0])
    stream_rows, grad_rows = (stream[0], cotangent[0])
    pack_ids = lax.dynamic_index_in_dim(segments, lax.axis_index("dp"), 0, keepdims=False)
    own_ids = lax.dynamic_slice_in_dim(pack_ids, seq_place * frames, frames)
    key_ids = jnp.roll(pack_ids, -seq_place * frames)

    pairs = shifted_copies(jnp.concatenate([key_rows, value_rows], 1), "seq")
    all_pairs = jnp.concatenate(pairs, 0)
    query_heads = split_heads(query_rows)
    key_heads = split_heads(all_pairs[:, :width])
    value_heads = split_heads(all_pairs[:, width:])
    scores = (
        jnp.einsum("hqe,hke->hqk", query_heads, key_heads, preferred_element_type=jnp.float32)
        * scale
    )
    scores = jnp.where((own_ids[:, None] == key_ids[None, :])[None], scores, MASKED)
    highest = jnp.max(scores, -1, keepdims=True)
    raised = jnp.exp(scores - highest)
    weights = raised * (1.0 / jnp.sum(raised, -1, keepdims=True))
    weights_low = weights.astype(jnp.bfloat16)
    mixed = merge_heads(
        jnp.einsum(
            "hqk,hke->hqe", weights_low, value_heads, preferred_element_type=jnp.float32
        ).astype(jnp.bfloat16)
    )
    hidden = stream_rows.astype(jnp.float32) + jnp.dot(
        mixed, attn_out, preferred_element_type=jnp.float32
    )
    normed_in, hat_in, inv_in = layer_norm(hidden, norm_gain)
    both = jnp.dot(normed_in.astype(jnp.bfloat16), point_in, preferred_element_type=jnp.float32)
    linear = both[:, :width]
    logistic = jax.nn.sigmoid(both[:, width:])
    conv_in = (linear * logistic).astype(jnp.bfloat16)
    taps = kernel.shape[0]
    reach = taps // 2
    padded = extended(conv_in, (("seq", 0),), reach)
    padded_ids = lax.dynamic_slice_in_dim(
        jnp.pad(pack_ids, reach, constant_values=-1), seq_place * frames, frames + 2 * reach
    )
    table = tap_table(padded_ids, own_ids, taps)
    conv_out = depthwise(padded, kernel, table)
    normed_out, hat_out, inv_out = layer_norm(conv_out, conv_gain)
    activated = (normed_out * jax.nn.sigmoid(normed_out)).astype(jnp.bfloat16)
    out_sum = Reduction(activated, grad_rows)
    act_grad = times_transposed(grad_rows, point_out)
    conv_grad = norm_backward(act_grad * swish_slope(normed_out), hat_out, inv_out, conv_gain)
    grad_padded = extended(conv_grad.astype(jnp.bfloat16), (("seq", 0),), reach).astype(
        conv_grad.dtype
    )
    tap_part = jnp.pad(tap_sums(conv_grad, padded, table), ((0, -taps % 16), (0, 0)))
    grad_padded = out_sum.tie(grad_padded)
    out_sum.step()
    in_grad = depthwise(grad_padded, kernel[::-1], table)
    both_grad = jnp.concatenate(
        [in_grad * logistic, in_grad * linear * logistic * (1.0 - logistic)], 1
    ).astype(jnp.bfloat16)
    back_in = times_transposed(both_grad, point_in)
    stream_out = (
        grad_rows.astype(jnp.float32) + norm_backward(back_in, hat_in, inv_in, norm_gain)
    ).astype(jnp.bfloat16)
    mixed_grad = times_transposed(stream_out, attn_out).astype(jnp.bfloat16)
    mixed_grad = out_sum.tie(mixed_grad)
    out_sum.step()
    grad_heads = split_heads(mixed_grad)
    slope = jnp.einsum(
        "hqe,hke->hqk", grad_heads, value_heads, preferred_element_type=jnp.float32
    )
    delta = jnp.sum(weights * slope, -1, keepdims=True)
    score_grad = (weights * (slope - delta)).astype(jnp.bfloat16)
    score_grad = out_sum.tie(score_grad)
    out_sum.step()
    query_grad = merge_heads(
        (
            jnp.einsum("hqk,hke->hqe", score_grad, key_heads, preferred_element_type=jnp.float32)
            * scale
        ).astype(jnp.bfloat16)
    )
    key_part = merge_heads(
        jnp.einsum("hqk,hqe->hke", score_grad, query_heads, preferred_element_type=jnp.float32)
        * scale
    )
    value_part = merge_heads(
        jnp.einsum("hqk,hqe->hke", weights_low, grad_heads, preferred_element_type=jnp.float32)
    )
    pair_part = jnp.concatenate([key_part, value_part], 1)
    pair_grad = returned(
        [pair_part[step * frames : (step + 1) * frames] for step in range(seq_count)], "seq"
    ).astype(jnp.bfloat16)
    first_routed = route(jnp.concatenate([stream_out, query_grad], 1), plan)
    in_sum = Reduction(mixed, stream_out, tap_part)
    second_spread = in_sum.tie(spread_rows(pair_grad))
    second_routed = collected(second_spread, plan)
    in_part = in_sum.finish()
    return (
        first_routed[None, :, width:],
        second_routed[None, :, :width],
        second_routed[None, :, width:],
        first_routed[None, :, :width],
        in_sum.extra[:taps],
        jnp.concatenate([in_part, out_sum.finish()], 1),
    )


def solution(mesh):
    placed = (
        P("dp", "seq", None),
        P("dp", "seq", None),
        P("dp", "seq", None),
        P("dp", "seq", None),
        P("dp", "seq", None),
        P(),
        P(),
        P(),
        P(),
        P(),
        P(),
        P(),
        P(),
    )
    return jax.shard_map(
        per_device,
        mesh=mesh,
        in_specs=placed,
        out_specs=(
            P("dp", "seq", None),
            P("dp", "seq", None),
            P("dp", "seq", None),
            P("dp", "seq", None),
            P(),
            P(("dp", "seq"), None),
        ),
        check_vma=False,
    )
```

```python
import jax
import jax.numpy as jnp
from jax import lax
from jax.sharding import PartitionSpec as P

HEAD_DIM = 64


EPSILON = 1e-05
MASKED = -1e30


def extended(cells, sides, width):
    for axis, dim in sides:
        count = lax.axis_size(axis)
        ends = count - 1
        head = lax.slice_in_dim(cells, 0, width, axis=dim)
        tail = lax.slice_in_dim(cells, cells.shape[dim] - width, cells.shape[dim], axis=dim)
        cells = jnp.concatenate(
            [
                lax.ppermute(tail, axis, [(i, (i + 1) % count) for i in range(ends)]),
                cells,
                lax.ppermute(head, axis, [((i + 1) % count, i) for i in range(ends)]),
            ],
            axis=dim,
        )
    return cells


def layer_norm(stream, gain):
    center = jnp.mean(stream, -1, keepdims=True)
    shifted = stream - center
    inverse = lax.rsqrt(jnp.mean(shifted * shifted, -1, keepdims=True) + EPSILON)
    normed = shifted * inverse
    return (normed * gain, normed, inverse)


def norm_backward(upstream, normed, inverse, gain):
    scaled = upstream * gain
    return inverse * (
        scaled
        - jnp.mean(scaled, -1, keepdims=True)
        - normed * jnp.mean(scaled * normed, -1, keepdims=True)
    )


def swish_slope(values):
    logistic = jax.nn.sigmoid(values)
    return logistic * (1.0 + values * (1.0 - logistic))


def tap_table(padded_ids, own_ids, taps):
    length = own_ids.shape[0]
    return (
        jnp.stack([padded_ids[tap : tap + length] for tap in range(taps)], 1) == own_ids[:, None]
    ).astype(jnp.float32)


def depthwise(padded, weights, table):
    length = table.shape[0]
    total = jnp.zeros((length, padded.shape[1]), jnp.float32)
    for tap in range(weights.shape[0]):
        total = (
            total
            + weights[tap].astype(jnp.float32)
            * padded[tap : tap + length].astype(jnp.float32)
            * table[:, tap : tap + 1]
        )
    return total


def tap_sums(upstream, padded, table):
    length = table.shape[0]
    return jnp.stack(
        [
            jnp.sum(
                upstream * padded[tap : tap + length].astype(jnp.float32) * table[:, tap : tap + 1],
                0,
            )
            for tap in range(table.shape[1])
        ]
    )


def times_transposed(left, right):
    return lax.dot_general(
        left, right, (((1,), (1,)), ((), ())), preferred_element_type=jnp.float32
    )


def transposed_times(left, right):
    return lax.dot_general(
        left, right, (((0,), (0,)), ((), ())), preferred_element_type=jnp.float32
    )


def split_heads(matrix):
    return matrix.reshape(matrix.shape[0], -1, HEAD_DIM).transpose(1, 0, 2)


def merge_heads(tensor):
    return tensor.transpose(1, 0, 2).reshape(tensor.shape[1], -1)


def shifted_copies(cells, axis):
    count = lax.axis_size(axis)
    return [cells] + [
        lax.ppermute(cells, axis, [((i + step) % count, i) for i in range(count)])
        for step in range(1, count)
    ]


def returned(parts, axis):
    count = lax.axis_size(axis)
    total = parts[0]
    for step in range(1, count):
        back = lax.ppermute(
            parts[step].astype(jnp.bfloat16),
            axis,
            [(i, (i + step) % count) for i in range(count)],
        )
        total = total + back.astype(jnp.float32)
    return total


def spread_rows(matrix):
    return lax.all_to_all(matrix, "dp", split_axis=0, concat_axis=0, tiled=True)


def collected(spread, plan):
    rows, width = spread.shape
    arranged = jnp.take(spread.reshape(plan.shape[0], -1, width), plan, axis=0, mode="clip")
    return spread_rows(arranged.reshape(rows, width))


def route(matrix, plan):
    return collected(spread_rows(matrix), plan)


def exchange_order():
    slots = (lax.axis_size("dp") - 1).bit_length()
    seqs = (lax.axis_size("seq") - 1).bit_length()
    return (
        [("dp", bit, seqs + bit) for bit in range(min(1, slots))]
        + [("seq", bit, bit) for bit in range(seqs)]
        + [("dp", bit, seqs + bit) for bit in range(1, slots)]
    )


def swapped(cells, axis, bit):
    return lax.ppermute(
        cells, axis, [(i, i ^ (1 << bit)) for i in range(lax.axis_size(axis))]
    )


def half_of(cells, dim, low, which):
    shape = cells.shape
    split = cells.reshape(shape[:dim] + (-1, 2, low) + shape[dim + 1 :])
    chosen = lax.dynamic_index_in_dim(split, which, dim + 1, keepdims=False)
    return chosen.reshape(shape[:dim] + (-1,) + shape[dim + 1 :])


def joined(axis, bit, outgoing, extra):
    outgoing = outgoing.astype(jnp.bfloat16)
    if extra is None:
        return swapped(outgoing, axis, bit).astype(jnp.float32), None
    rounded = lax.reduce_precision(extra, 8, 7)
    arrived = swapped(
        jnp.concatenate([outgoing, rounded.astype(jnp.bfloat16)], 0), axis, bit
    ).astype(jnp.float32)
    count = outgoing.shape[0]
    return arrived[:count], rounded + arrived[count:]


class Reduction:
    def __init__(self, left, right, extra=None):
        self.order = exchange_order()
        self.rows = left.shape[1] >> len(self.order)
        self.positions = sorted(position for _, _, position in self.order)
        self.extra = extra
        axis, bit, low, mine = self.next_exchange()
        outgoing = transposed_times(half_of(left, 1, low, 1 - mine), right)
        arrived, self.extra = joined(axis, bit, outgoing, self.extra)
        self.total = transposed_times(half_of(left, 1, low, mine), right) + arrived

    def next_exchange(self):
        axis, bit, position = self.order.pop(0)
        low = self.rows << self.positions.index(position)
        self.positions.remove(position)
        return axis, bit, low, (lax.axis_index(axis) >> bit) & 1

    def step(self):
        if self.order:
            axis, bit, low, mine = self.next_exchange()
            outgoing = half_of(self.total, 0, low, 1 - mine)
            arrived, self.extra = joined(axis, bit, outgoing, self.extra)
            self.total = half_of(self.total, 0, low, mine) + arrived

    def finish(self):
        while self.order:
            self.step()
        return self.total

    def tie(self, other):
        self.total, other = lax.optimization_barrier((self.total, other))
        return other


def per_device(
    queries,
    keys,
    values,
    stream,
    cotangent,
    attn_out,
    point_in,
    kernel,
    point_out,
    norm_gain,
    conv_gain,
    segments,
    plan,
):
    frames, width = (queries.shape[1], queries.shape[2])
    seq_place = lax.axis_index("seq")
    seq_count = lax.axis_size("seq")
    scale = HEAD_DIM ** (-0.5)
    query_rows, key_rows, value_rows = (queries[0], keys[0], values[0])
    stream_rows, grad_rows = (stream[0], cotangent[0])
    pack_ids = lax.dynamic_index_in_dim(segments, lax.axis_index("dp"), 0, keepdims=False)
    own_ids = lax.dynamic_slice_in_dim(pack_ids, seq_place * frames, frames)
    key_ids = jnp.roll(pack_ids, -seq_place * frames)

    pairs = shifted_copies(jnp.concatenate([key_rows, value_rows], 1), "seq")
    all_pairs = jnp.concatenate(pairs, 0)
    query_heads = split_heads(query_rows)
    key_heads = split_heads(all_pairs[:, :width])
    value_heads = split_heads(all_pairs[:, width:])
    scores = (
        jnp.einsum("hqe,hke->hqk", query_heads, key_heads, preferred_element_type=jnp.float32)
        * scale
    )
    scores = jnp.where((own_ids[:, None] == key_ids[None, :])[None], scores, MASKED)
    highest = jnp.max(scores, -1, keepdims=True)
    raised = jnp.exp(scores - highest)
    weights = raised * (1.0 / jnp.sum(raised, -1, keepdims=True))
    weights_low = weights.astype(jnp.bfloat16)
    mixed = merge_heads(
        jnp.einsum(
            "hqk,hke->hqe", weights_low, value_heads, preferred_element_type=jnp.float32
        ).astype(jnp.bfloat16)
    )
    hidden = stream_rows.astype(jnp.float32) + jnp.dot(
        mixed, attn_out, preferred_element_type=jnp.float32
    )
    normed_in, hat_in, inv_in = layer_norm(hidden, norm_gain)
    both = jnp.dot(normed_in.astype(jnp.bfloat16), point_in, preferred_element_type=jnp.float32)
    linear = both[:, :width]
    logistic = jax.nn.sigmoid(both[:, width:])
    conv_in = (linear * logistic).astype(jnp.bfloat16)
    taps = kernel.shape[0]
    reach = taps // 2
    padded = extended(conv_in, (("seq", 0),), reach)
    padded_ids = lax.dynamic_slice_in_dim(
        jnp.pad(pack_ids, reach, constant_values=-1), seq_place * frames, frames + 2 * reach
    )
    table = tap_table(padded_ids, own_ids, taps)
    conv_out = depthwise(padded, kernel, table)
    normed_out, hat_out, inv_out = layer_norm(conv_out, conv_gain)
    activated = (normed_out * jax.nn.sigmoid(normed_out)).astype(jnp.bfloat16)
    out_sum = Reduction(activated, grad_rows)
    act_grad = times_transposed(grad_rows, point_out)
    conv_grad = norm_backward(act_grad * swish_slope(normed_out), hat_out, inv_out, conv_gain)
    grad_padded = extended(conv_grad.astype(jnp.bfloat16), (("seq", 0),), reach).astype(
        conv_grad.dtype
    )
    tap_part = jnp.pad(tap_sums(conv_grad, padded, table), ((0, -taps % 16), (0, 0)))
    grad_padded = out_sum.tie(grad_padded)
    out_sum.step()
    in_grad = depthwise(grad_padded, kernel[::-1], table)
    both_grad = jnp.concatenate(
        [in_grad * logistic, in_grad * linear * logistic * (1.0 - logistic)], 1
    ).astype(jnp.bfloat16)
    back_in = times_transposed(both_grad, point_in)
    stream_out = (
        grad_rows.astype(jnp.float32) + norm_backward(back_in, hat_in, inv_in, norm_gain)
    ).astype(jnp.bfloat16)
    mixed_grad = times_transposed(stream_out, attn_out).astype(jnp.bfloat16)
    grad_heads = split_heads(mixed_grad)
    slope = jnp.einsum(
        "hqe,hke->hqk", grad_heads, value_heads, preferred_element_type=jnp.float32
    )
    delta = jnp.sum(weights * slope, -1, keepdims=True)
    score_grad = (weights * (slope - delta)).astype(jnp.bfloat16)
    score_grad = out_sum.tie(score_grad)
    out_sum.step()
    query_grad = merge_heads(
        (
            jnp.einsum("hqk,hke->hqe", score_grad, key_heads, preferred_element_type=jnp.float32)
            * scale
        ).astype(jnp.bfloat16)
    )
    key_part = merge_heads(
        jnp.einsum("hqk,hqe->hke", score_grad, query_heads, preferred_element_type=jnp.float32)
        * scale
    )
    value_part = merge_heads(
        jnp.einsum("hqk,hqe->hke", weights_low, grad_heads, preferred_element_type=jnp.float32)
    )
    pair_part = jnp.concatenate([key_part, value_part], 1)
    first_spread = spread_rows(jnp.concatenate([stream_out, query_grad], 1))
    in_sum = Reduction(mixed, stream_out, tap_part)
    pair_grad = returned(
        [pair_part[step * frames : (step + 1) * frames] for step in range(seq_count)], "seq"
    ).astype(jnp.bfloat16)
    pair_grad, first_spread, in_sum.total, in_sum.extra, out_sum.total = (
        lax.optimization_barrier(
            (pair_grad, first_spread, in_sum.total, in_sum.extra, out_sum.total)
        )
    )
    in_sum.step()
    out_sum.step()
    second_spread = spread_rows(pair_grad)
    first_routed = collected(first_spread, plan)
    second_spread = in_sum.tie(second_spread)
    in_sum.step()
    second_routed = collected(second_spread, plan)
    in_part = in_sum.finish()
    return (
        first_routed[None, :, width:],
        second_routed[None, :, :width],
        second_routed[None, :, width:],
        first_routed[None, :, :width],
        in_sum.extra[:taps],
        jnp.concatenate([in_part, out_sum.finish()], 1),
    )


def solution(mesh):
    placed = (
        P("dp", "seq", None),
        P("dp", "seq", None),
        P("dp", "seq", None),
        P("dp", "seq", None),
        P("dp", "seq", None),
        P(),
        P(),
        P(),
        P(),
        P(),
        P(),
        P(),
        P(),
    )
    return jax.shard_map(
        per_device,
        mesh=mesh,
        in_specs=placed,
        out_specs=(
            P("dp", "seq", None),
            P("dp", "seq", None),
            P("dp", "seq", None),
            P("dp", "seq", None),
            P(),
            P(("dp", "seq"), None),
        ),
        check_vma=False,
    )
```

```python
import jax
import jax.numpy as jnp
from jax import lax
from jax.sharding import PartitionSpec as P

HEAD_DIM = 64


EPSILON = 1e-05
MASKED = -1e30


def extended(cells, sides, width):
    for axis, dim in sides:
        count = lax.axis_size(axis)
        ends = count - 1
        head = lax.slice_in_dim(cells, 0, width, axis=dim)
        tail = lax.slice_in_dim(cells, cells.shape[dim] - width, cells.shape[dim], axis=dim)
        cells = jnp.concatenate(
            [
                lax.ppermute(tail, axis, [(i, (i + 1) % count) for i in range(ends)]),
                cells,
                lax.ppermute(head, axis, [((i + 1) % count, i) for i in range(ends)]),
            ],
            axis=dim,
        )
    return cells


def layer_norm(stream, gain):
    center = jnp.mean(stream, -1, keepdims=True)
    shifted = stream - center
    inverse = lax.rsqrt(jnp.mean(shifted * shifted, -1, keepdims=True) + EPSILON)
    normed = shifted * inverse
    return (normed * gain, normed, inverse)


def norm_backward(upstream, normed, inverse, gain):
    scaled = upstream * gain
    return inverse * (
        scaled
        - jnp.mean(scaled, -1, keepdims=True)
        - normed * jnp.mean(scaled * normed, -1, keepdims=True)
    )


def swish_slope(values):
    logistic = jax.nn.sigmoid(values)
    return logistic * (1.0 + values * (1.0 - logistic))


def tap_table(padded_ids, own_ids, taps):
    length = own_ids.shape[0]
    return (
        jnp.stack([padded_ids[tap : tap + length] for tap in range(taps)], 1) == own_ids[:, None]
    ).astype(jnp.float32)


def depthwise(padded, weights, table):
    length = table.shape[0]
    total = jnp.zeros((length, padded.shape[1]), jnp.float32)
    for tap in range(weights.shape[0]):
        total = (
            total
            + weights[tap].astype(jnp.float32)
            * padded[tap : tap + length].astype(jnp.float32)
            * table[:, tap : tap + 1]
        )
    return total


def tap_sums(upstream, padded, table):
    length = table.shape[0]
    return jnp.stack(
        [
            jnp.sum(
                upstream * padded[tap : tap + length].astype(jnp.float32) * table[:, tap : tap + 1],
                0,
            )
            for tap in range(table.shape[1])
        ]
    )


def times_transposed(left, right):
    return lax.dot_general(
        left, right, (((1,), (1,)), ((), ())), preferred_element_type=jnp.float32
    )


def transposed_times(left, right):
    return lax.dot_general(
        left, right, (((0,), (0,)), ((), ())), preferred_element_type=jnp.float32
    )


def split_heads(matrix):
    return matrix.reshape(matrix.shape[0], -1, HEAD_DIM).transpose(1, 0, 2)


def merge_heads(tensor):
    return tensor.transpose(1, 0, 2).reshape(tensor.shape[1], -1)


def shifted_copies(cells, axis):
    count = lax.axis_size(axis)
    return [cells] + [
        lax.ppermute(cells, axis, [((i + step) % count, i) for i in range(count)])
        for step in range(1, count)
    ]


def returned(parts, axis):
    count = lax.axis_size(axis)
    total = parts[0]
    for step in range(1, count):
        back = lax.ppermute(
            parts[step].astype(jnp.bfloat16),
            axis,
            [(i, (i + step) % count) for i in range(count)],
        )
        total = total + back.astype(jnp.float32)
    return total


def spread_rows(matrix):
    return lax.all_to_all(matrix, "dp", split_axis=0, concat_axis=0, tiled=True)


def by_slot(spread, plan):
    rows, width = spread.shape
    arranged = jnp.take(spread.reshape(plan.shape[0], -1, width), plan, axis=0, mode="clip")
    return arranged.reshape(rows, width)


def exchange_order():
    slots = (lax.axis_size("dp") - 1).bit_length()
    seqs = (lax.axis_size("seq") - 1).bit_length()
    return (
        [("dp", bit, seqs + bit) for bit in range(min(1, slots))]
        + [("seq", bit, bit) for bit in range(seqs)]
        + [("dp", bit, seqs + bit) for bit in range(1, slots)]
    )


def swapped(cells, axis, bit):
    return lax.ppermute(
        cells, axis, [(i, i ^ (1 << bit)) for i in range(lax.axis_size(axis))]
    )


def half_of(cells, dim, low, which):
    shape = cells.shape
    split = cells.reshape(shape[:dim] + (-1, 2, low) + shape[dim + 1 :])
    chosen = lax.dynamic_index_in_dim(split, which, dim + 1, keepdims=False)
    return chosen.reshape(shape[:dim] + (-1,) + shape[dim + 1 :])


def joined(axis, bit, outgoing, extra):
    outgoing = outgoing.astype(jnp.bfloat16)
    if extra is None:
        return swapped(outgoing, axis, bit).astype(jnp.float32), None
    rounded = lax.reduce_precision(extra, 8, 7)
    arrived = swapped(
        jnp.concatenate([outgoing, rounded.astype(jnp.bfloat16)], 0), axis, bit
    ).astype(jnp.float32)
    count = outgoing.shape[0]
    return arrived[:count], rounded + arrived[count:]


class Reduction:
    def __init__(self, left, right, extra=None):
        self.order = exchange_order()
        self.rows = left.shape[1] >> len(self.order)
        self.positions = sorted(position for _, _, position in self.order)
        self.extra = extra
        axis, bit, low, mine = self.next_exchange()
        outgoing = transposed_times(half_of(left, 1, low, 1 - mine), right)
        arrived, self.extra = joined(axis, bit, outgoing, self.extra)
        self.total = transposed_times(half_of(left, 1, low, mine), right) + arrived

    def next_exchange(self):
        axis, bit, position = self.order.pop(0)
        low = self.rows << self.positions.index(position)
        self.positions.remove(position)
        return axis, bit, low, (lax.axis_index(axis) >> bit) & 1

    def step(self):
        if self.order:
            axis, bit, low, mine = self.next_exchange()
            outgoing = half_of(self.total, 0, low, 1 - mine)
            arrived, self.extra = joined(axis, bit, outgoing, self.extra)
            self.total = half_of(self.total, 0, low, mine) + arrived

    def finish(self):
        while self.order:
            self.step()
        return self.total

    def tie(self, other):
        self.total, other = lax.optimization_barrier((self.total, other))
        return other


def per_device(
    queries,
    keys,
    values,
    stream,
    cotangent,
    attn_out,
    point_in,
    kernel,
    point_out,
    norm_gain,
    conv_gain,
    segments,
    plan,
):
    frames, width = (queries.shape[1], queries.shape[2])
    seq_place = lax.axis_index("seq")
    seq_count = lax.axis_size("seq")
    scale = HEAD_DIM ** (-0.5)
    query_rows, key_rows, value_rows = (queries[0], keys[0], values[0])
    stream_rows, grad_rows = (stream[0], cotangent[0])
    pack_ids = lax.dynamic_index_in_dim(segments, lax.axis_index("dp"), 0, keepdims=False)
    own_ids = lax.dynamic_slice_in_dim(pack_ids, seq_place * frames, frames)
    key_ids = jnp.roll(pack_ids, -seq_place * frames)

    pairs = shifted_copies(jnp.concatenate([key_rows, value_rows], 1), "seq")
    all_pairs = jnp.concatenate(pairs, 0)
    query_heads = split_heads(query_rows)
    key_heads = split_heads(all_pairs[:, :width])
    value_heads = split_heads(all_pairs[:, width:])
    scores = (
        jnp.einsum("hqe,hke->hqk", query_heads, key_heads, preferred_element_type=jnp.float32)
        * scale
    )
    scores = jnp.where((own_ids[:, None] == key_ids[None, :])[None], scores, MASKED)
    highest = jnp.max(scores, -1, keepdims=True)
    raised = jnp.exp(scores - highest)
    weights = raised * (1.0 / jnp.sum(raised, -1, keepdims=True))
    weights_low = weights.astype(jnp.bfloat16)
    mixed = merge_heads(
        jnp.einsum(
            "hqk,hke->hqe", weights_low, value_heads, preferred_element_type=jnp.float32
        ).astype(jnp.bfloat16)
    )
    hidden = stream_rows.astype(jnp.float32) + jnp.dot(
        mixed, attn_out, preferred_element_type=jnp.float32
    )
    normed_in, hat_in, inv_in = layer_norm(hidden, norm_gain)
    both = jnp.dot(normed_in.astype(jnp.bfloat16), point_in, preferred_element_type=jnp.float32)
    linear = both[:, :width]
    logistic = jax.nn.sigmoid(both[:, width:])
    conv_in = (linear * logistic).astype(jnp.bfloat16)
    taps = kernel.shape[0]
    reach = taps // 2
    padded = extended(conv_in, (("seq", 0),), reach)
    padded_ids = lax.dynamic_slice_in_dim(
        jnp.pad(pack_ids, reach, constant_values=-1), seq_place * frames, frames + 2 * reach
    )
    table = tap_table(padded_ids, own_ids, taps)
    conv_out = depthwise(padded, kernel, table)
    normed_out, hat_out, inv_out = layer_norm(conv_out, conv_gain)
    activated = (normed_out * jax.nn.sigmoid(normed_out)).astype(jnp.bfloat16)
    out_sum = Reduction(activated, grad_rows)
    act_grad = times_transposed(grad_rows, point_out)
    conv_grad = norm_backward(act_grad * swish_slope(normed_out), hat_out, inv_out, conv_gain)
    grad_padded = extended(conv_grad.astype(jnp.bfloat16), (("seq", 0),), reach).astype(
        conv_grad.dtype
    )
    tap_part = jnp.pad(tap_sums(conv_grad, padded, table), ((0, -taps % 16), (0, 0)))
    grad_padded = out_sum.tie(grad_padded)
    out_sum.step()
    in_grad = depthwise(grad_padded, kernel[::-1], table)
    both_grad = jnp.concatenate(
        [in_grad * logistic, in_grad * linear * logistic * (1.0 - logistic)], 1
    ).astype(jnp.bfloat16)
    back_in = times_transposed(both_grad, point_in)
    stream_out = (
        grad_rows.astype(jnp.float32) + norm_backward(back_in, hat_in, inv_in, norm_gain)
    ).astype(jnp.bfloat16)
    mixed_grad = times_transposed(stream_out, attn_out).astype(jnp.bfloat16)
    grad_heads = split_heads(mixed_grad)
    slope = jnp.einsum(
        "hqe,hke->hqk", grad_heads, value_heads, preferred_element_type=jnp.float32
    )
    delta = jnp.sum(weights * slope, -1, keepdims=True)
    score_grad = (weights * (slope - delta)).astype(jnp.bfloat16)
    score_grad = out_sum.tie(score_grad)
    out_sum.step()
    query_grad = merge_heads(
        (
            jnp.einsum("hqk,hke->hqe", score_grad, key_heads, preferred_element_type=jnp.float32)
            * scale
        ).astype(jnp.bfloat16)
    )
    key_part = merge_heads(
        jnp.einsum("hqk,hqe->hke", score_grad, query_heads, preferred_element_type=jnp.float32)
        * scale
    )
    value_part = merge_heads(
        jnp.einsum("hqk,hqe->hke", weights_low, grad_heads, preferred_element_type=jnp.float32)
    )
    pair_part = jnp.concatenate([key_part, value_part], 1)
    first_spread = spread_rows(jnp.concatenate([stream_out, query_grad], 1))
    in_sum = Reduction(mixed, stream_out, tap_part)
    pair_grad = returned(
        [pair_part[step * frames : (step + 1) * frames] for step in range(seq_count)], "seq"
    ).astype(jnp.bfloat16)
    pair_grad, first_spread, in_sum.total, in_sum.extra, out_sum.total = (
        lax.optimization_barrier(
            (pair_grad, first_spread, in_sum.total, in_sum.extra, out_sum.total)
        )
    )
    in_sum.step()
    out_sum.step()
    second_spread = spread_rows(pair_grad)
    first_slots = by_slot(first_spread, plan)
    second_spread = in_sum.tie(second_spread)
    in_sum.step()
    routed = spread_rows(jnp.concatenate([first_slots, by_slot(second_spread, plan)], 1))
    in_part = in_sum.finish()
    return (
        routed[None, :, width : 2 * width],
        routed[None, :, 2 * width : 3 * width],
        routed[None, :, 3 * width :],
        routed[None, :, :width],
        in_sum.extra[:taps],
        jnp.concatenate([in_part, out_sum.finish()], 1),
    )


def solution(mesh):
    placed = (
        P("dp", "seq", None),
        P("dp", "seq", None),
        P("dp", "seq", None),
        P("dp", "seq", None),
        P("dp", "seq", None),
        P(),
        P(),
        P(),
        P(),
        P(),
        P(),
        P(),
        P(),
    )
    return jax.shard_map(
        per_device,
        mesh=mesh,
        in_specs=placed,
        out_specs=(
            P("dp", "seq", None),
            P("dp", "seq", None),
            P("dp", "seq", None),
            P("dp", "seq", None),
            P(),
            P(("dp", "seq"), None),
        ),
        check_vma=False,
    )
```
